256 devices in a mesh: row: 8 (over y, core), col: 4 (over x), layer: 8 (over z).
Axes of the slice: x: 4, y: 4, z: 8, core: 2. Of those that a mesh axis runs over, the one named last changes fastest.
Arguments:
- a_vals: bfloat16 [192, 8, 8, 64, 128], P('row', 'layer', 'col'), may hold values from -0.375 to 0.375
- a_cols: int32 [192, 8, 8, 2], P('row', 'layer', 'col'), may hold values from 0 to 7, as said below
- a_count: int32 [192, 8, 8], P('row', 'layer', 'col'), may hold values from 0 to 2, as said below
- panel_map: int32 [8, 8], replicated, may hold values from 0 to 7, each once within a row
- p_vals: bfloat16 [8, 8, 8, 4, 64, 256], P('layer', 'row', None, 'col'), may hold values from -6 to 6
- p_cols: int32 [8, 8, 8, 4, 4], P('layer', 'row', None, 'col'), may hold values from 0 to 7, as said below
- p_count: int32 [8, 8, 8, 4], P('layer', 'row', None, 'col'), may hold values from 0 to 4, as said below
Outputs:
- product: bfloat16 [12288, 2048], P(('row', 'col', 'layer'))
The draws below stay inside these ranges and needn't reach their ends.
Inputs may be any that keep to these rules, and one draw needn't show every extreme that they name: `a_count`: each block row has at most 27 valid operator blocks in all, some block row exactly 27, and some entry reaches 2. `a_cols`: the slots of one block row and section name distinct block columns. `p_cols`: the slots of one block row and group name distinct coarse columns. `p_count`: reaches 4 somewhere in every draw.
All inputs are finite; a program needn't handle non-finite values.
Results may differ from the reference program's by a relative error of at most 0.001.
Values may be sent and summed in bfloat16 or wider, within the bound.
No kernel may reach another device: no remote copies, remote signals or barrier semaphores. Data moves between devices by JAX's collectives and lax.ppermute only.
A program may use at most 128 MiB of HBM per device.

```python
import jax
import jax.numpy as jnp
from jax import lax

B = 64
NST = 8
SA = 2
SP = 4
CB = 8
PW = 8
NBR = 192
N_COL = 4
N_LAYER = 8


def draw_a_count(key, part):
    slot_total = N_LAYER * NST * SA
    section_total = N_LAYER * NST
    keys = jax.random.split(jax.random.fold_in(key, 11), NBR)
    orders = jax.vmap(lambda single: jax.random.permutation(single, slot_total))(keys)
    heavy = jax.random.randint(jax.random.fold_in(key, 12), (NBR,), 0, 4) == 0
    position = jax.random.randint(jax.random.fold_in(key, 13), (), 0, NBR)
    forced = jnp.arange(NBR, dtype=jnp.int32) == position
    orders = jnp.where(forced[:, None], jnp.arange(slot_total, dtype=jnp.int32)[None, :], orders)
    light = jax.random.randint(jax.random.fold_in(key, 14), (NBR,), 12, 28)
    taken_count = jnp.where(heavy | forced, 27, light)
    taken = jnp.arange(slot_total, dtype=jnp.int32)[None, :] < taken_count[:, None]
    section_of = orders // SA
    hits = (section_of[:, :, None] == jnp.arange(section_total, dtype=jnp.int32)[None, None, :]) & taken[:, :, None]
    counts = jnp.sum(hits.astype(jnp.int32), axis=1)
    return counts.reshape(NBR, N_LAYER, NST).astype(jnp.int32)


def draw_a_cols(key, part):
    total = NBR * N_LAYER * NST
    keys = jax.random.split(jax.random.fold_in(key, 41), total)
    chosen = jax.vmap(lambda single: jax.random.permutation(single, PW)[:SA])(keys)
    return chosen.reshape(NBR, N_LAYER, NST, SA).astype(jnp.int32)


def draw_p_cols(key, part):
    total = N_LAYER * NST * PW * N_COL
    keys = jax.random.split(jax.random.fold_in(key, 21), total)
    chosen = jax.vmap(lambda single: jax.random.permutation(single, CB)[:SP])(keys)
    return chosen.reshape(N_LAYER, NST, PW, N_COL, SP).astype(jnp.int32)


def draw_p_count(key, part):
    total = N_LAYER * NST * PW * N_COL
    base_count = jax.random.randint(jax.random.fold_in(key, 31), (total,), 0, SP // 2 + 1)
    position = jax.random.randint(jax.random.fold_in(key, 32), (), 0, total)
    filled = jnp.where(jnp.arange(total, dtype=jnp.int32) == position, SP, base_count)
    return filled.reshape(N_LAYER, NST, PW, N_COL).astype(jnp.int32)


def steps_of(key, shape, cuts, low, top_value):
    def one(dim, parts):
        heights = jax.random.uniform(jax.random.fold_in(jax.random.fold_in(key, 6), dim), (parts,), jnp.float32, low / len(cuts), top_value / len(cuts))
        return jnp.repeat(jnp.exp(heights), shape[dim] // parts).reshape((-1,) + (1,) * (len(shape) - dim - 1))

    loudness = one(*cuts[0])
    for cut in cuts[1:]:
        loudness = loudness * one(*cut)
    return loudness


def gaussian(key, dims, width, most, pieces=(), kind=jnp.bfloat16):
    gain = steps_of(key, dims, pieces, -0.22, 0.18) if pieces else 1.0
    drawn = jax.random.normal(key, dims, jnp.float32) * width * gain
    return jnp.minimum(jnp.maximum(drawn, -most), most).astype(kind)


def setup_inputs(seed: int = 0) -> dict:
    key_of = jax.random.split(jax.random.key(seed), 8)
    return {
        "a_vals": gaussian(key_of[0], (NBR, N_LAYER, NST, B, SA * B), (4 * B) ** -0.5, 0.375, ((0, 8), (1, 8), (2, 4))),
        "a_cols": draw_a_cols(jax.random.fold_in(key_of[7], 71), 0),
        "a_count": draw_a_count(jax.random.fold_in(key_of[7], 71), 0),
        "panel_map": jax.vmap(lambda own: jax.random.permutation(own, NST))(jax.random.split(key_of[3], N_LAYER)).reshape((N_LAYER, NST)).astype(jnp.int32),
        "p_vals": gaussian(key_of[4], (N_LAYER, NST, PW, N_COL, B, SP * B), 1.0, 6.0, ((0, 8), (1, 8), (3, 4))),
        "p_cols": draw_p_cols(jax.random.fold_in(key_of[7], 71), 0),
        "p_count": draw_p_count(jax.random.fold_in(key_of[7], 71), 0),
    }


def reference(a_vals, a_cols, a_count, panel_map, p_vals, p_cols, p_count):
    block_side = a_vals.shape[3]
    slot_a = a_cols.shape[3]
    slot_p = p_cols.shape[4]
    layers = panel_map.shape[0]
    sections = panel_map.shape[1]
    p_width = p_vals.shape[2]
    groups = p_vals.shape[3]
    flat_rows = layers * sections * p_width
    p_flat = p_vals.reshape(flat_rows, groups, block_side, slot_p, block_side)
    pcol_flat = p_cols.reshape(flat_rows, groups, slot_p)
    pcount_flat = p_count.reshape(flat_rows, groups)
    panel_base = (jnp.arange(layers, dtype=jnp.int32)[:, None] * sections + panel_map.astype(jnp.int32)) * p_width

    def one_row(inputs):
        row_vals, row_cols, row_count = inputs
        a_blocks = row_vals.astype(jnp.float32).reshape(layers, sections, block_side, slot_a, block_side)
        a_mask = (jnp.arange(slot_a, dtype=jnp.int32)[None, None, :] < row_count[:, :, None]).astype(jnp.float32)
        a_blocks = a_blocks * a_mask[:, :, None, :, None]
        k_index = (panel_base[:, :, None] + row_cols).astype(jnp.int32)
        p_blocks = p_flat[k_index].astype(jnp.float32)
        p_mask = (jnp.arange(slot_p, dtype=jnp.int32) < pcount_flat[k_index][..., None]).astype(jnp.float32)
        onehot = (pcol_flat[k_index][..., None] == jnp.arange(CB, dtype=jnp.int32)).astype(jnp.float32) * p_mask[..., None]
        products = jnp.einsum("lsxay,lsagytz->lsagtxz", a_blocks, p_blocks, precision=lax.Precision.HIGHEST)
        row_out = jnp.einsum("lsagtxz,lsagtc->xgcz", products, onehot, precision=lax.Precision.HIGHEST)
        return row_out.reshape(block_side, groups * CB * block_side)

    stacked = lax.map(one_row, (a_vals, a_cols, a_count))
    return stacked.reshape(-1, groups * CB * block_side).astype(jnp.bfloat16)
```

```python
import functools

import jax
import jax.numpy as jnp
from jax import lax
from jax.experimental import pallas as pl
from jax.experimental.pallas import tpu as pltpu
from jax.sharding import PartitionSpec as P

CB = 8
BF = jnp.bfloat16
F32 = jnp.float32


def expand_kernel(col_ref, p_ref, out_ref):
    lane = lax.broadcasted_iota(jnp.int32, (16, 128), 1)
    low = lane < 64
    panel_rows = p_ref.shape[1] // 64

    @pl.loop(0, p_ref.shape[0])
    def _(q):
        @pl.loop(0, panel_rows, unroll=2)
        def _(w):
            k = q * panel_rows + w
            blocks = p_ref[q, pl.ds(pl.multiple_of(w * 64, 64), 64), :]
            sources, wanted = [], []
            for half in range(2):
                straight = blocks[:, half * 128:(half + 1) * 128]
                swapped = jnp.concatenate([straight[:, 64:], straight[:, :64]], axis=1)
                left = col_ref[k, 2 * half]
                right = col_ref[k, 2 * half + 1]
                sources += [straight.reshape(4, 16, 128), swapped.reshape(4, 16, 128)]
                wanted += [jnp.where(low, left, right - 1), jnp.where(low, right, left - 1)]
            for j in range(4):
                total = None
                for source, want in zip(sources, wanted):
                    term = source * jnp.where(want == 2 * j, 1.0, 0.0).astype(BF)[None]
                    total = term if total is None else total + term
                out_ref[k, j] = total.reshape(64, 128)

    out_ref[p_ref.shape[0] * panel_rows] = jnp.zeros(out_ref.shape[1:], BF)


def product_kernel(k_ref, *refs):
    a_refs, dense_ref, out_ref = refs[:-2], refs[-2], refs[-1]
    step = pl.program_id(0)
    sections = a_refs[0].shape[1]
    for u in range(6):
        i = step * 6 + u
        left, right = [], []
        for n, a_ref in enumerate(a_refs):
            for s in range(sections):
                left.append(a_ref[u, s])
                for slot in range(2):
                    k = k_ref[n, (i * sections + s) * 2 + slot]
                    right.append(jnp.concatenate([dense_ref[k, j] for j in range(4)], axis=1))
        total = jnp.dot(
            jnp.concatenate(left, axis=1), jnp.concatenate(right, axis=0), preferred_element_type=F32
        )
        for piece in range(4):
            row = u * 64 + piece * 16
            out_ref[row // 48, 0, row % 48:row % 48 + 16, :] = total[piece * 16:(piece + 1) * 16]


def split_kernel(c_ref, y_ref, *outs):
    for s, out in enumerate(outs):
        out[...] = y_ref[lax.rem(c_ref[0] + s, len(outs))].astype(BF)


def join_kernel(c_ref, *refs):
    pieces, out = refs[:-1], refs[-1]
    for s, piece in enumerate(pieces):
        width = piece.shape[1]
        source = lax.rem(c_ref[0] + len(pieces) - s, len(pieces))
        out[:, pl.ds(pl.multiple_of(source * width, width), width)] = piece[...]


VMEM_SPEC = pl.BlockSpec(memory_space=pltpu.VMEM)
SMEM_SPEC = pl.BlockSpec(memory_space=pltpu.SMEM)


def body(cols, a_vals, a_cols, a_count, panel_map, p_vals, p_cols, p_count):
    rows = a_vals.shape[0]
    sections = a_vals.shape[2]
    side = a_vals.shape[3]
    here = lax.axis_index("col")
    layer_map = lax.dynamic_index_in_dim(panel_map, lax.axis_index("layer"), 0, keepdims=False)
    panels = lax.dynamic_slice_in_dim(layer_map, here * sections, sections, 0)
    panel_rows = p_vals.shape[2]
    fine = panel_map.shape[1] * panel_rows

    slot_p = p_cols.shape[4]
    p_index = jnp.where(jnp.arange(slot_p) < p_count[0, 0, :, 0, None], p_cols[0, 0, :, 0], -9)
    p_flat = p_vals.reshape(panel_rows * side, slot_p * side)
    p_extra = jnp.pad(p_index.reshape(1, -1).astype(BF), ((0, 15), (0, slot_p * side - p_index.size)))
    p_all = lax.all_gather(jnp.concatenate([p_flat, p_extra], axis=0), "row", axis=0)
    p_col_all = p_all[:, panel_rows * side, :p_index.size].astype(jnp.int32).reshape(fine, slot_p)

    slot_a = a_cols.shape[3]
    k_index = jnp.where(
        jnp.arange(slot_a) < a_count[:, 0, :, None],
        panels[None, :, None] * panel_rows + a_cols[:, 0],
        fine,
    ).reshape(1, -1)
    mine = a_vals[:, 0]
    parts, indices = [mine], [k_index]
    for s in range(1, cols):
        to = [(n, (n + s) % cols) for n in range(cols)]
        indices.append(lax.ppermute(k_index, "col", to))
        parts.append(lax.ppermute(mine, "col", to))
    k_all = jnp.concatenate(indices, axis=0)

    dense = pl.pallas_call(
        expand_kernel,
        out_shape=jax.ShapeDtypeStruct((fine + 1, 4, side, 128), BF),
        in_specs=[SMEM_SPEC, VMEM_SPEC],
        out_specs=VMEM_SPEC,
        name="expand",
        cost_estimate=pl.CostEstimate(flops=0, bytes_accessed=6 << 20, transcendentals=0),
    )(p_col_all, p_all)

    width = CB * side
    groups = rows // 6
    partial_sum = pl.pallas_call(
        product_kernel,
        out_shape=jax.ShapeDtypeStruct((8, groups, 48, width), F32),
        grid_spec=pltpu.PrefetchScalarGridSpec(
            num_scalar_prefetch=1,
            grid=(groups,),
            in_specs=[pl.BlockSpec((6, sections, side, 128), lambda g, k: (g, 0, 0, 0))] * cols
            + [pl.BlockSpec((fine + 1, 4, side, 128), lambda g, k: (0, 0, 0, 0), pipeline_mode=pl.Buffered(1))],
            out_specs=pl.BlockSpec((8, 1, 48, width), lambda g, k: (0, g, 0, 0)),
        ),
        name="product",
        compiler_params=pltpu.CompilerParams(vmem_limit_bytes=48 << 20),
        cost_estimate=pl.CostEstimate(flops=2 * rows * side * 1024 * width, bytes_accessed=11 << 20, transcendentals=0),
    )(k_all, *parts, dense)

    mine_sum = lax.psum_scatter(partial_sum, "layer", scatter_dimension=0, tiled=True)[0]
    where = here.reshape(1)
    pieces = pl.pallas_call(
        split_kernel,
        out_shape=[jax.ShapeDtypeStruct((48, width), BF)] * cols,
        in_specs=[SMEM_SPEC, VMEM_SPEC],
        out_specs=[VMEM_SPEC] * cols,
        name="split",
    )(where, mine_sum)
    arrived = [pieces[0]]
    for s in range(1, cols):
        arrived.append(lax.ppermute(pieces[s], "col", [(n, (n + s) % cols) for n in range(cols)]))
    return pl.pallas_call(
        join_kernel,
        out_shape=jax.ShapeDtypeStruct((48, cols * width), BF),
        in_specs=[SMEM_SPEC] + [VMEM_SPEC] * cols,
        out_specs=VMEM_SPEC,
        name="join",
    )(where, *arrived)


def solution(mesh):
    placed = (
        P("row", "layer", "col", None, None),
        P("row", "layer", "col", None),
        P("row", "layer", "col"),
        P(),
        P("layer", "row", None, "col", None, None),
        P("layer", "row", None, "col", None),
        P("layer", "row", None, "col"),
    )
    return jax.shard_map(
        functools.partial(body, mesh.shape["col"]),
        mesh=mesh,
        in_specs=placed,
        out_specs=P(("row", "col", "layer"), None),
        check_vma=False,
    )
```

```python
import functools

import jax
import jax.numpy as jnp
from jax import lax
from jax.experimental import pallas as pl
from jax.experimental.pallas import tpu as pltpu
from jax.sharding import PartitionSpec as P

CB = 8
PANEL_ROWS = 8
BF = jnp.bfloat16
F32 = jnp.float32
VMEM_SPEC = pl.BlockSpec(memory_space=pltpu.VMEM)
SMEM_SPEC = pl.BlockSpec(memory_space=pltpu.SMEM)


def expand_kernel(core, row_ref, p_ref, *refs):
    out_ref = refs[-1]
    panels = out_ref.shape[0] // PANEL_ROWS
    row = row_ref[0]

    @pl.loop(0, p_ref.shape[0])
    def _(n):
        away = jnp.where(n == 0, 0, jnp.where(n == 1, panels - 2, jnp.where(n == 2, 2, 4)))
        panel = lax.rem(row + away, panels)
        if core:
            panel = panel + 1 - 2 * lax.rem(panel, 2)
        for w in range(PANEL_ROWS):
            blocks = p_ref[n, w * 64:(w + 1) * 64, :]
            sources, wanted = [], []
            for half in range(2):
                straight = blocks[:, half * 128:(half + 1) * 128]
                swapped = jnp.concatenate([straight[:, 64:], straight[:, :64]], axis=1)
                for side, source in enumerate((straight, swapped)):
                    sources.append(source.reshape(4, 16, 128))
                    r = PANEL_ROWS * 64 + 2 * w + half
                    want = p_ref[n, r:r + 1, side * 128:(side + 1) * 128]
                    wanted.append(jnp.broadcast_to(want.astype(F32), (16, 128)))
            for j in range(4):
                total = None
                for source, want in zip(sources, wanted):
                    term = source * jnp.where(want == 2.0 * j, 1.0, 0.0).astype(BF)[None]
                    total = term if total is None else total + term
                out_ref[panel * PANEL_ROWS + w, j] = total.reshape(64, 128)

    if core:
        out_ref[panels * PANEL_ROWS] = jnp.zeros(out_ref.shape[1:], BF)


def product_kernel(half, layers, here_ref, *refs):
    a_refs, k_far_ref, dense_ref = refs[:4], refs[4], refs[5]
    outs, (sums, k_vector, k_ref, sem) = refs[6:-4], refs[-4:]
    count = a_refs[0].shape[0] - 16
    for n in range(3):
        k_vector[n:n + 1] = a_refs[n][count:count + 1].astype(F32).astype(jnp.int32)
    k_vector[3:4] = k_far_ref[0:1].astype(F32).astype(jnp.int32)
    copy = pltpu.make_async_copy(k_vector, k_ref, sem)
    copy.start()
    copy.wait()
    sections = 2
    groups = sums.shape[1]
    for g in range(groups):
        @pl.loop(0, 2)
        def _(h):
            for v in range(3):
                u = h * 3 + v
                r = g * 6 + u
                i = half * groups * 6 + r
                left, right = [], []
                for n, a_ref in enumerate(a_refs):
                    for s in range(sections):
                        first = ((r if n == 3 else i) * sections + s) * 64
                        left.append(a_ref[pl.ds(pl.multiple_of(first, 64), 64), :])
                        for slot in range(2):
                            k = k_ref[n, (i * sections + s) * 2 + slot]
                            right.append(jnp.concatenate([dense_ref[k, j] for j in range(4)], axis=1))
                total = jnp.dot(
                    jnp.concatenate(left, axis=1), jnp.concatenate(right, axis=0), preferred_element_type=F32
                )
                for piece in range(4):
                    row = v * 64 + piece * 16
                    sums[h * 4 + row // 48, g, row % 48:row % 48 + 16, :] = total[piece * 16:(piece + 1) * 16]
    for o, out in enumerate(outs):
        out[...] = sums[lax.rem(here_ref[0] + o, layers)]


def split_kernel(c_ref, *refs):
    ins, outs, sums = refs[:6], refs[6:-1], refs[-1]
    for h in range(2):
        sums[2 * h:2 * h + 2] = ins[3 * h][...] + ins[3 * h + 1][...] + ins[3 * h + 2][...]
    for s, out in enumerate(outs):
        out[...] = sums[lax.rem(c_ref[0] + s, len(outs))].astype(BF)


def join_kernel(c_ref, *refs):
    pieces, out = refs[:-1], refs[-1]
    for s, piece in enumerate(pieces):
        width = piece.shape[1]
        source = lax.rem(c_ref[0] + len(pieces) - s, len(pieces))
        out[:, pl.ds(pl.multiple_of(source * width, width), width)] = piece[...]


def shift(x, axis, size, by):
    return lax.ppermute(x, axis, [(n, (n + by) % size) for n in range(size)])


def body(a_vals, a_cols, a_count, panel_map, p_vals, p_cols, p_count):
    rows = a_vals.shape[0]
    sections = a_vals.shape[2]
    side = a_vals.shape[3]
    cols, layers, grid_rows = 4, 8, 8
    here = lax.axis_index("col")
    layer = lax.axis_index("layer")
    row = lax.axis_index("row")
    layer_map = lax.dynamic_index_in_dim(panel_map, layer, 0, keepdims=False)
    panels = lax.dynamic_slice_in_dim(layer_map, here * sections, sections, 0)
    panel_rows = p_vals.shape[2]
    fine = panel_map.shape[1] * panel_rows

    slot_a = a_cols.shape[3]
    k_index = jnp.where(
        jnp.arange(slot_a) < a_count[:, 0, :, None],
        panels[None, :, None] * panel_rows + a_cols[:, 0],
        fine,
    ).reshape(1, -1)
    k_tile = jnp.pad(k_index.astype(BF), ((0, 15), (0, 2 * side - k_index.size)))
    own = jnp.concatenate([a_vals[:, 0].reshape(rows * sections * side, 2 * side), k_tile], axis=0)
    from_left, from_right = shift(own, "col", cols, 1), shift(own, "col", cols, -1)

    slot_p = p_cols.shape[4]
    index = jnp.where(jnp.arange(slot_p) < p_count[0, 0, :, 0, None], p_cols[0, 0, :, 0], -9)
    odd = index.reshape(panel_rows, 2, 2)
    odd = jnp.concatenate([odd - jnp.array([0, 1]), odd[:, :, ::-1] - jnp.array([0, 1])], axis=2)
    wanted = jnp.broadcast_to(odd[:, :, :, None].astype(BF), (panel_rows, 2, 4, side))
    mine = jnp.concatenate(
        [p_vals.reshape(panel_rows * side, slot_p * side), wanted.reshape(2 * panel_rows, 4 * side)], axis=0
    )
    p_line = [shift(mine, "row", grid_rows, by) for by in (2, -2, 4)]
    p_line, from_left, from_right = lax.optimization_barrier((p_line, from_left, from_right))
    p_line = jnp.stack([mine] + p_line)
    p_pair = lax.ppermute(p_line, "row", [(n, n ^ 1) for n in range(grid_rows)])

    cut = rows * sections * side // 2
    far_first = shift(from_left[:cut], "col", cols, 1)
    far_second = shift(from_right[cut:], "col", cols, -1)
    far = [far_first, far_second[:cut]]
    k_far = far_second[cut:]

    dense = []
    for core, part in enumerate((p_line, p_pair)):
        dense = [pl.pallas_call(
            functools.partial(expand_kernel, core),
            out_shape=jax.ShapeDtypeStruct((fine + 1, 4, side, 128), BF),
            in_specs=[SMEM_SPEC] + [VMEM_SPEC] * (1 + core),
            out_specs=VMEM_SPEC,
            input_output_aliases={2: 0} if core else {},
            name="expand",
            compiler_params=pltpu.CompilerParams(vmem_limit_bytes=14 << 20),
            cost_estimate=pl.CostEstimate(flops=0, bytes_accessed=10 << 20, transcendentals=0),
        )(row.reshape(1), part, *dense)]
    dense = dense[0]

    width = CB * side
    groups = rows // 12
    block = (groups, 48, width)
    finals = []
    for half in range(2):
        part = pl.pallas_call(
            functools.partial(product_kernel, half, layers),
            out_shape=[jax.ShapeDtypeStruct(block, F32)] * layers,
            in_specs=[SMEM_SPEC] + [VMEM_SPEC] * 6,
            out_specs=[VMEM_SPEC] * layers,
            scratch_shapes=[
                pltpu.VMEM((layers,) + block, F32),
                pltpu.VMEM((8, 128), jnp.int32),
                pltpu.SMEM((8, 128), jnp.int32),
                pltpu.SemaphoreType.DMA(()),
            ],
            name="product",
            compiler_params=pltpu.CompilerParams(vmem_limit_bytes=16 << 20),
            cost_estimate=pl.CostEstimate(flops=rows * side * 1024 * width, bytes_accessed=8 << 20, transcendentals=0),
        )(layer.reshape(1), own, from_left, from_right, far[half], k_far, dense)
        reach = 4 if half == 0 else 3
        up, down = part[reach], part[reach + 1]
        for step in range(4):
            if step < reach:
                up = shift(up, "layer", layers, 1)
                if step < reach - 1:
                    up = up + part[reach - 1 - step]
            if step < 7 - reach:
                down = shift(down, "layer", layers, -1)
                if step < 6 - reach:
                    down = down + part[reach + 2 + step]
        finals += [part[0], up, down]

    where = here.reshape(1)
    pieces = pl.pallas_call(
        split_kernel,
        out_shape=[jax.ShapeDtypeStruct((48, width), BF)] * cols,
        in_specs=[SMEM_SPEC] + [VMEM_SPEC] * 6,
        out_specs=[VMEM_SPEC] * cols,
        scratch_shapes=[pltpu.VMEM((cols, 48, width), F32)],
        name="split",
        compiler_params=pltpu.CompilerParams(vmem_limit_bytes=4 << 20),
    )(where, *finals)
    arrived = [pieces[0]] + [shift(pieces[s], "col", cols, s) for s in range(1, cols)]
    return pl.pallas_call(
        join_kernel,
        out_shape=jax.ShapeDtypeStruct((48, cols * width), BF),
        in_specs=[SMEM_SPEC] + [VMEM_SPEC] * cols,
        out_specs=VMEM_SPEC,
        name="join",
        compiler_params=pltpu.CompilerParams(vmem_limit_bytes=2 << 20),
    )(where, *arrived)


def solution(mesh):
    placed = (
        P("row", "layer", "col", None, None),
        P("row", "layer", "col", None),
        P("row", "layer", "col"),
        P(),
        P("layer", "row", None, "col", None, None),
        P("layer", "row", None, "col", None),
        P("layer", "row", None, "col"),
    )
    return jax.shard_map(
        body,
        mesh=mesh,
        in_specs=placed,
        out_specs=P(("row", "col", "layer"), None),
        check_vma=False,
    )
```

```python
import functools

import jax
import jax.numpy as jnp
from jax import lax
from jax.experimental import pallas as pl
from jax.experimental.pallas import tpu as pltpu
from jax.sharding import PartitionSpec as P

CB = 8
PANEL_ROWS = 8
BF = jnp.bfloat16
F32 = jnp.float32
VMEM_SPEC = pl.BlockSpec(memory_space=pltpu.VMEM)
SMEM_SPEC = pl.BlockSpec(memory_space=pltpu.SMEM)


def expand_kernel(core, row_ref, p_ref, *refs):
    out_ref = refs[-1]
    panels = out_ref.shape[0] // PANEL_ROWS
    row = row_ref[0]

    @pl.loop(0, p_ref.shape[0])
    def _(n):
        panel = row ^ (2 * n + core)
        for w in range(PANEL_ROWS):
            blocks = p_ref[n, w * 64:(w + 1) * 64, :]
            sources, wanted = [], []
            for half in range(2):
                straight = blocks[:, half * 128:(half + 1) * 128]
                swapped = jnp.concatenate([straight[:, 64:], straight[:, :64]], axis=1)
                for side, source in enumerate((straight, swapped)):
                    sources.append(source.reshape(4, 16, 128))
                    r = PANEL_ROWS * 64 + 2 * w + half
                    want = p_ref[n, r:r + 1, side * 128:(side + 1) * 128]
                    wanted.append(jnp.broadcast_to(want.astype(F32), (16, 128)))
            for j in range(4):
                total = None
                for source, want in zip(sources, wanted):
                    term = source * jnp.where(want == 2.0 * j, 1.0, 0.0).astype(BF)[None]
                    total = term if total is None else total + term
                out_ref[panel * PANEL_ROWS + w, j] = total.reshape(64, 128)

    if core:
        out_ref[panels * PANEL_ROWS] = jnp.zeros(out_ref.shape[1:], BF)


def multiply(sums, add, k_ref, dense_ref, lefts):
    for g in range(sums.shape[1]):
        @pl.loop(0, 2)
        def _(h):
            for v in range(3):
                i = g * 6 + h * 3 + v
                left, right = [], []
                for n, (a_ref, base) in enumerate(lefts(g)):
                    for s in range(2):
                        first = ((i - base) * 2 + s) * 64
                        left.append(a_ref[pl.ds(pl.multiple_of(first, 64), 64), :])
                        for slot in range(2):
                            k = k_ref[n, (i * 2 + s) * 2 + slot]
                            right.append(jnp.concatenate([dense_ref[k, j] for j in range(4)], axis=1))
                total = jnp.dot(
                    jnp.concatenate(left, axis=1), jnp.concatenate(right, axis=0), preferred_element_type=F32
                )
                for piece in range(4):
                    row = v * 64 + piece * 16
                    where = (h * 4 + row // 48, g, slice(row % 48, row % 48 + 16))
                    term = total[piece * 16:(piece + 1) * 16]
                    sums[where] = sums[where] + term if add else term


def load_k(k_rows, k_vector, k_ref, sem):
    for n, k in enumerate(k_rows):
        k_vector[n:n + 1] = k.astype(F32).astype(jnp.int32)
    copy = pltpu.make_async_copy(k_vector, k_ref, sem)
    copy.start()
    copy.wait()


def near_kernel(*refs):
    a_refs, dense_ref, sums, scratch = refs[:3], refs[3], refs[4], refs[5:]
    count = a_refs[0].shape[0] - 16
    load_k([a[count:count + 1] for a in a_refs], *scratch)
    multiply(sums, False, scratch[1], dense_ref, lambda g: [(a, 0) for a in a_refs])


def code(x_of, out, scales):
    scales[...] = jnp.zeros_like(scales)
    for g in range(12):
        x = x_of(g)
        most = jnp.maximum(jnp.max(jnp.abs(x), axis=0, keepdims=True), 1e-33)
        e = jnp.ceil(64.0 * (jnp.log2(most) - 15.0)) + 1.0
        scales[g:g + 1] = e
        out[g * 16:(g + 1) * 16] = jnp.floor(x * jnp.exp2(e * (-1.0 / 64)) + 0.5).astype(jnp.int32).astype(jnp.int16)
    out[192:208] = scales[...].astype(jnp.int32).astype(jnp.int16)


def decoded(ref, scales):
    scales[...] = jnp.exp2(ref[192:208].astype(jnp.int32).astype(F32) * (1.0 / 64))
    return lambda g: ref[g * 16:(g + 1) * 16].astype(jnp.int32).astype(F32) * scales[g:g + 1]


def rows_of(sums, index):
    return lambda g: sums[index, g // 3, (g % 3) * 16:(g % 3) * 16 + 16, :]


def far_kernel(layer_ref, sums_in, first_ref, second_ref, dense_ref, sums, up, down, *scratch):
    count = second_ref.shape[0] - 16
    k_scratch, scales = scratch[:3], scratch[3]
    load_k([second_ref[count:count + 1]], *k_scratch)
    half = sums.shape[1] // 2
    multiply(
        sums, True, k_scratch[1], dense_ref,
        lambda g: [(first_ref, 0) if g < half else (second_ref, 6 * half)],
    )
    layers = sums.shape[0]
    code(rows_of(sums, lax.rem(layer_ref[0] + 4, layers)), up, scales)
    code(rows_of(sums, lax.rem(layer_ref[0] + 5, layers)), down, scales)


def hop_kernel(offset, layer_ref, arrived, sums, out, scales_in, scales):
    mine = rows_of(sums, lax.rem(layer_ref[0] + offset, sums.shape[0]))
    other = decoded(arrived, scales_in)
    code(lambda g: mine(g) + other(g), out, scales)


def split_kernel(here_ref, layer_ref, up, down, sums, *refs):
    outs, (whole, scales_up, scales_down) = refs[:-3], refs[-3:]
    mine = rows_of(sums, layer_ref[0])
    above, below = decoded(up, scales_up), decoded(down, scales_down)
    for g in range(12):
        whole[g // 3, (g % 3) * 16:(g % 3) * 16 + 16] = mine(g) + above(g) + below(g)
    for s, out in enumerate(outs):
        out[...] = whole[here_ref[0] ^ s].astype(BF)


def join_kernel(c_ref, *refs):
    pieces, out = refs[:-1], refs[-1]
    for s, piece in enumerate(pieces):
        width = piece.shape[1]
        source = c_ref[0] ^ s
        out[:, pl.ds(pl.multiple_of(source * width, width), width)] = piece[...]


def swap(x, axis, size, mask):
    return lax.ppermute(x, axis, [(n, n ^ mask) for n in range(size)])


def shift(x, axis, size, by):
    return lax.ppermute(x, axis, [(n, (n + by) % size) for n in range(size)])


def body(a_vals, a_cols, a_count, panel_map, p_vals, p_cols, p_count):
    rows = a_vals.shape[0]
    sections = a_vals.shape[2]
    side = a_vals.shape[3]
    cols, layers, grid_rows = 4, 8, 8
    here = lax.axis_index("col")
    layer = lax.axis_index("layer")
    row = lax.axis_index("row")
    layer_map = lax.dynamic_index_in_dim(panel_map, layer, 0, keepdims=False)
    panels = lax.dynamic_slice_in_dim(layer_map, here * sections, sections, 0)
    panel_rows = p_vals.shape[2]
    fine = panel_map.shape[1] * panel_rows

    slot_a = a_cols.shape[3]
    k_index = jnp.where(
        jnp.arange(slot_a) < a_count[:, 0, :, None],
        panels[None, :, None] * panel_rows + a_cols[:, 0],
        fine,
    ).reshape(1, -1)
    k_tile = jnp.pad(k_index.astype(BF), ((0, 15), (0, 2 * side - k_index.size)))
    own = jnp.concatenate([a_vals[:, 0].reshape(rows * sections * side, 2 * side), k_tile], axis=0)
    from_left, from_right = swap(own, "col", cols, 1), swap(own, "col", cols, 3)

    slot_p = p_cols.shape[4]
    index = jnp.where(jnp.arange(slot_p) < p_count[0, 0, :, 0, None], p_cols[0, 0, :, 0], -9)
    odd = index.reshape(panel_rows, 2, 2)
    odd = jnp.concatenate([odd - jnp.array([0, 1]), odd[:, :, ::-1] - jnp.array([0, 1])], axis=2)
    wanted = jnp.broadcast_to(odd[:, :, :, None].astype(BF), (panel_rows, 2, 4, side))
    mine = jnp.concatenate(
        [p_vals.reshape(panel_rows * side, slot_p * side), wanted.reshape(2 * panel_rows, 4 * side)], axis=0
    )
    p_line = [swap(mine, "row", grid_rows, mask) for mask in (2, 4, 6)]
    p_line, from_left, from_right = lax.optimization_barrier((p_line, from_left, from_right))
    p_line = jnp.stack([mine] + p_line)
    p_pair = swap(p_line, "row", grid_rows, 1)

    cut = rows * sections * side // 2
    far_first = swap(from_right[:cut], "col", cols, 1)
    far_second = swap(from_left[cut:], "col", cols, 3)

    dense = []
    for core, part in enumerate((p_line, p_pair)):
        dense = [pl.pallas_call(
            functools.partial(expand_kernel, core),
            out_shape=jax.ShapeDtypeStruct((fine + 1, 4, side, 128), BF),
            in_specs=[SMEM_SPEC] + [VMEM_SPEC] * (1 + core),
            out_specs=VMEM_SPEC,
            input_output_aliases={2: 0} if core else {},
            name="expand",
            compiler_params=pltpu.CompilerParams(vmem_limit_bytes=14 << 20),
            cost_estimate=pl.CostEstimate(flops=0, bytes_accessed=10 << 20, transcendentals=0),
        )(row.reshape(1), part, *dense)]
    dense = dense[0]

    width = CB * side
    sums_shape = jax.ShapeDtypeStruct((layers, rows // 6, 48, width), F32)
    coded = jax.ShapeDtypeStruct((208, width), jnp.int16)
    k_scratch = [pltpu.VMEM((8, 128), jnp.int32), pltpu.SMEM((8, 128), jnp.int32), pltpu.SemaphoreType.DMA(())]
    scales = pltpu.VMEM((16, width), F32)
    layer = layer.reshape(1)
    sums = pl.pallas_call(
        near_kernel,
        out_shape=sums_shape,
        in_specs=[VMEM_SPEC] * 4,
        out_specs=VMEM_SPEC,
        scratch_shapes=k_scratch,
        name="near",
        compiler_params=pltpu.CompilerParams(vmem_limit_bytes=14 << 20),
        cost_estimate=pl.CostEstimate(flops=4 << 30, bytes_accessed=11 << 20, transcendentals=0),
    )(own, from_left, from_right, dense)
    sums, up, down = pl.pallas_call(
        far_kernel,
        out_shape=[sums_shape, coded, coded],
        in_specs=[SMEM_SPEC] + [VMEM_SPEC] * 4,
        out_specs=[VMEM_SPEC] * 3,
        scratch_shapes=k_scratch + [scales],
        input_output_aliases={1: 0},
        name="far",
        compiler_params=pltpu.CompilerParams(vmem_limit_bytes=14 << 20),
        cost_estimate=pl.CostEstimate(flops=1 << 30, bytes_accessed=9 << 20, transcendentals=0),
    )(layer, sums, far_first, far_second, dense)

    def hop(offset, arrived):
        return pl.pallas_call(
            functools.partial(hop_kernel, offset),
            out_shape=coded,
            in_specs=[SMEM_SPEC] + [VMEM_SPEC] * 2,
            out_specs=VMEM_SPEC,
            scratch_shapes=[scales, scales],
            name="hop",
            compiler_params=pltpu.CompilerParams(vmem_limit_bytes=4 << 20),
            cost_estimate=pl.CostEstimate(flops=0, bytes_accessed=1 << 20, transcendentals=0),
        )(layer, arrived, sums)

    for step in range(4):
        up = shift(up, "layer", layers, 1)
        if step < 3:
            up = hop(3 - step, up)
            down = shift(down, "layer", layers, -1)
        if step < 2:
            down = hop(6 + step, down)

    where = here.reshape(1)
    pieces = pl.pallas_call(
        split_kernel,
        out_shape=[jax.ShapeDtypeStruct((48, width), BF)] * cols,
        in_specs=[SMEM_SPEC] * 2 + [VMEM_SPEC] * 3,
        out_specs=[VMEM_SPEC] * cols,
        scratch_shapes=[pltpu.VMEM((cols, 48, width), F32), scales, scales],
        name="split",
        compiler_params=pltpu.CompilerParams(vmem_limit_bytes=4 << 20),
    )(where, layer, up, down, sums)
    arrived = [pieces[0]] + [swap(pieces[s], "col", cols, s) for s in range(1, cols)]
    return pl.pallas_call(
        join_kernel,
        out_shape=jax.ShapeDtypeStruct((48, cols * width), BF),
        in_specs=[SMEM_SPEC] + [VMEM_SPEC] * cols,
        out_specs=VMEM_SPEC,
        name="join",
        compiler_params=pltpu.CompilerParams(vmem_limit_bytes=2 << 20),
    )(where, *arrived)


def solution(mesh):
    placed = (
        P("row", "layer", "col", None, None),
        P("row", "layer", "col", None),
        P("row", "layer", "col"),
        P(),
        P("layer", "row", None, "col", None, None),
        P("layer", "row", None, "col", None),
        P("layer", "row", None, "col"),
    )
    return jax.shard_map(
        body,
        mesh=mesh,
        in_specs=placed,
        out_specs=P(("row", "col", "layer"), None),
        check_vma=False,
    )
```

```python
import functools

import jax
import jax.numpy as jnp
from jax import lax
from jax.experimental import pallas as pl
from jax.experimental.pallas import tpu as pltpu
from jax.sharding import PartitionSpec as P

CB = 8
PANEL_ROWS = 8
BF = jnp.bfloat16
F32 = jnp.float32
VMEM_SPEC = pl.BlockSpec(memory_space=pltpu.VMEM)
SMEM_SPEC = pl.BlockSpec(memory_space=pltpu.SMEM)


def expand_kernel(row_ref, *refs):
    p_refs, out_ref = refs[:2], refs[2]
    panels = out_ref.shape[0] // PANEL_ROWS
    for core, p_ref in enumerate(p_refs):
        @pl.loop(0, p_ref.shape[0])
        def _(n):
            expand_panel(p_ref, n, row_ref[0] ^ (2 * n + core), out_ref)

    out_ref[panels * PANEL_ROWS] = jnp.zeros(out_ref.shape[1:], BF)


def expand_panel(p_ref, n, panel, out_ref):
    for w in range(PANEL_ROWS):
        blocks = p_ref[n, w * 64:(w + 1) * 64, :]
        sources, wanted = [], []
        for half in range(2):
            straight = blocks[:, half * 128:(half + 1) * 128]
            swapped = jnp.concatenate([straight[:, 64:], straight[:, :64]], axis=1)
            for side, source in enumerate((straight, swapped)):
                sources.append(source.reshape(4, 16, 128))
                r = PANEL_ROWS * 64 + 2 * w + half
                want = p_ref[n, r:r + 1, side * 128:(side + 1) * 128]
                wanted.append(jnp.broadcast_to(want.astype(F32), (16, 128)))
        for j in range(4):
            total = None
            for source, want in zip(sources, wanted):
                term = source * jnp.where(want == 2.0 * j, 1.0, 0.0).astype(BF)[None]
                total = term if total is None else total + term
            out_ref[panel * PANEL_ROWS + w, j] = total.reshape(64, 128)


def multiply(sums, add, k_ref, dense_ref, lefts):
    for g in range(sums.shape[1]):
        @pl.loop(0, 2)
        def _(h):
            for v in range(3):
                i = g * 6 + h * 3 + v
                left, right = [], []
                for n, (a_ref, base) in enumerate(lefts(g)):
                    for s in range(2):
                        first = ((i - base) * 2 + s) * 64
                        left.append(a_ref[pl.ds(pl.multiple_of(first, 64), 64), :])
                        for slot in range(2):
                            k = k_ref[4 * n + 2 * s + slot, i]
                            right.append(jnp.concatenate([dense_ref[k, j] for j in range(4)], axis=1))
                total = jnp.dot(
                    jnp.concatenate(left, axis=1), jnp.concatenate(right, axis=0), preferred_element_type=F32
                )
                for piece in range(4):
                    row = v * 64 + piece * 16
                    where = (h * 4 + row // 48, g, slice(row % 48, row % 48 + 16))
                    term = total[piece * 16:(piece + 1) * 16]
                    sums[where] = sums[where] + term if add else term


def load_k(k_tiles, k_vector, k_ref, sem):
    for n, k in enumerate(k_tiles):
        k_vector[4 * n:4 * n + 4] = k.astype(F32).astype(jnp.int32)[0:4]
    copy = pltpu.make_async_copy(k_vector, k_ref, sem)
    copy.start()
    copy.wait()


def near_kernel(*refs):
    a_refs, dense_ref, sums, scratch = refs[:3], refs[3], refs[4], refs[5:]
    count = a_refs[0].shape[0] - 16
    load_k([a[count:count + 16] for a in a_refs], *scratch)
    multiply(sums, False, scratch[1], dense_ref, lambda g: [(a, 0) for a in a_refs])


def code(x_of, out, scales):
    scales[...] = jnp.zeros_like(scales)
    for g in range(12):
        x = x_of(g)
        most = jnp.maximum(jnp.max(jnp.abs(x), axis=0, keepdims=True), 1e-33)
        e = jnp.ceil(64.0 * (jnp.log2(most) - 15.0)) + 1.0
        scales[g:g + 1] = e
        out[g * 16:(g + 1) * 16] = jnp.floor(x * jnp.exp2(e * (-1.0 / 64)) + 0.5).astype(jnp.int32).astype(jnp.int16)
    out[192:208] = scales[...].astype(jnp.int32).astype(jnp.int16)


def decoded(ref, scales):
    scales[...] = jnp.exp2(ref[192:208].astype(jnp.int32).astype(F32) * (1.0 / 64))
    return lambda g: ref[g * 16:(g + 1) * 16].astype(jnp.int32).astype(F32) * scales[g:g + 1]


def rows_of(sums, index):
    return lambda g: sums[index, g // 3, (g % 3) * 16:(g % 3) * 16 + 16, :]


def far_kernel(layer_ref, sums_in, first_ref, second_ref, dense_ref, sums, up, down, *scratch):
    count = second_ref.shape[0] - 16
    k_scratch, scales = scratch[:3], scratch[3]
    load_k([second_ref[count:count + 16]], *k_scratch)
    half = sums.shape[1] // 2
    multiply(
        sums, True, k_scratch[1], dense_ref,
        lambda g: [(first_ref, 0) if g < half else (second_ref, 6 * half)],
    )
    layers = sums.shape[0]
    code(rows_of(sums, lax.rem(layer_ref[0] + 4, layers)), up, scales)
    code(rows_of(sums, lax.rem(layer_ref[0] + 5, layers)), down, scales)


def hop_kernel(offset, layer_ref, arrived, sums, out, scales_in, scales):
    mine = rows_of(sums, lax.rem(layer_ref[0] + offset, sums.shape[0]))
    other = decoded(arrived, scales_in)
    code(lambda g: mine(g) + other(g), out, scales)


def split_kernel(here_ref, layer_ref, up, down, sums, *refs):
    outs, (whole, scales_up, scales_down) = refs[:-3], refs[-3:]
    mine = rows_of(sums, layer_ref[0])
    above, below = decoded(up, scales_up), decoded(down, scales_down)
    for g in range(12):
        whole[g // 3, (g % 3) * 16:(g % 3) * 16 + 16] = mine(g) + above(g) + below(g)
    for s, out in enumerate(outs):
        out[...] = whole[here_ref[0] ^ s].astype(BF)


def join_kernel(c_ref, *refs):
    pieces, out = refs[:-1], refs[-1]
    for s, piece in enumerate(pieces):
        width = piece.shape[1]
        source = c_ref[0] ^ s
        out[:, pl.ds(pl.multiple_of(source * width, width), width)] = piece[...]


def swap(x, axis, size, mask):
    return lax.ppermute(x, axis, [(n, n ^ mask) for n in range(size)])


def shift(x, axis, size, by):
    return lax.ppermute(x, axis, [(n, (n + by) % size) for n in range(size)])


def body(a_vals, a_cols, a_count, panel_map, p_vals, p_cols, p_count):
    rows = a_vals.shape[0]
    sections = a_vals.shape[2]
    side = a_vals.shape[3]
    cols, layers, grid_rows = 4, 8, 8
    here = lax.axis_index("col")
    layer = lax.axis_index("layer")
    row = lax.axis_index("row")
    panel_rows = p_vals.shape[2]
    fine = panel_map.shape[1] * panel_rows

    a_flat = a_vals[:, 0].reshape(rows * sections * side, 2 * side)
    p_flat = p_vals.reshape(panel_rows * side, p_cols.shape[4] * side)
    panels = lax.dynamic_slice(panel_map, (layer, here * sections), (1, sections)).reshape(sections, 1, 1)
    slot_a = a_cols.shape[3]
    valid = jnp.arange(slot_a)[None, :, None] < a_count.transpose(1, 2, 0)[0][:, None, :]
    k_index = jnp.where(valid, panels * panel_rows + a_cols.transpose(1, 2, 3, 0)[0], fine)
    k_tile = jnp.pad(
        k_index.astype(BF).reshape(sections * slot_a, rows), ((0, 16 - sections * slot_a), (0, 2 * side - rows))
    )
    own = jnp.concatenate([a_flat, k_tile], axis=0)

    from_left, from_right = swap(own, "col", cols, 1), swap(own, "col", cols, 3)

    slot_p = p_cols.shape[4]
    index = jnp.where(jnp.arange(slot_p) < p_count[0, 0, :, 0, None], p_cols[0, 0, :, 0], -9)
    odd = index.reshape(panel_rows, 2, 2)
    odd = jnp.concatenate([odd - jnp.array([0, 1]), odd[:, :, ::-1] - jnp.array([0, 1])], axis=2)
    wanted = jnp.broadcast_to(odd[:, :, :, None].astype(BF), (panel_rows, 2, 4, side))
    mine = jnp.concatenate([p_flat, wanted.reshape(2 * panel_rows, 4 * side)], axis=0)
    p_line = [swap(mine, "row", grid_rows, mask) for mask in (2, 4, 6)]
    cut = a_flat.shape[0] // 2
    halves = [from_right[:cut], from_left[cut:]]
    p_line, halves, from_left, from_right = lax.optimization_barrier((p_line, halves, from_left, from_right))
    far_first, far_second = swap(halves[0], "col", cols, 1), swap(halves[1], "col", cols, 3)
    p_line = jnp.stack([mine] + p_line)
    p_pair = swap(p_line, "row", grid_rows, 1)

    dense = pl.pallas_call(
        expand_kernel,
        out_shape=jax.ShapeDtypeStruct((fine + 1, 4, side, 128), BF),
        in_specs=[SMEM_SPEC] + [VMEM_SPEC] * 2,
        out_specs=VMEM_SPEC,
        name="expand",
        compiler_params=pltpu.CompilerParams(vmem_limit_bytes=14 << 20),
        cost_estimate=pl.CostEstimate(flops=0, bytes_accessed=10 << 20, transcendentals=0),
    )(row.reshape(1), p_line, p_pair)

    width = CB * side
    sums_shape = jax.ShapeDtypeStruct((layers, rows // 6, 48, width), F32)
    coded = jax.ShapeDtypeStruct((208, width), jnp.int16)
    k_scratch = [pltpu.VMEM((16, 128), jnp.int32), pltpu.SMEM((16, 128), jnp.int32), pltpu.SemaphoreType.DMA(())]
    scales = pltpu.VMEM((16, width), F32)
    layer = layer.reshape(1)
    sums = pl.pallas_call(
        near_kernel,
        out_shape=sums_shape,
        in_specs=[VMEM_SPEC] * 4,
        out_specs=VMEM_SPEC,
        scratch_shapes=k_scratch,
        name="near",
        compiler_params=pltpu.CompilerParams(vmem_limit_bytes=14 << 20),
        cost_estimate=pl.CostEstimate(flops=4 << 30, bytes_accessed=11 << 20, transcendentals=0),
    )(own, from_left, from_right, dense)
    sums, up, down = pl.pallas_call(
        far_kernel,
        out_shape=[sums_shape, coded, coded],
        in_specs=[SMEM_SPEC] + [VMEM_SPEC] * 4,
        out_specs=[VMEM_SPEC] * 3,
        scratch_shapes=k_scratch + [scales],
        input_output_aliases={1: 0},
        name="far",
        compiler_params=pltpu.CompilerParams(vmem_limit_bytes=14 << 20),
        cost_estimate=pl.CostEstimate(flops=1 << 30, bytes_accessed=9 << 20, transcendentals=0),
    )(layer, sums, far_first, far_second, dense)

    def hop(offset, arrived):
        return pl.pallas_call(
            functools.partial(hop_kernel, offset),
            out_shape=coded,
            in_specs=[SMEM_SPEC] + [VMEM_SPEC] * 2,
            out_specs=VMEM_SPEC,
            scratch_shapes=[scales, scales],
            name="hop",
            compiler_params=pltpu.CompilerParams(vmem_limit_bytes=4 << 20),
            cost_estimate=pl.CostEstimate(flops=0, bytes_accessed=1 << 20, transcendentals=0),
        )(layer, arrived, sums)

    for step in range(4):
        up = shift(up, "layer", layers, 1)
        if step < 3:
            up = hop(3 - step, up)
            down = shift(down, "layer", layers, -1)
        if step < 2:
            down = hop(6 + step, down)

    where = here.reshape(1)
    pieces = pl.pallas_call(
        split_kernel,
        out_shape=[jax.ShapeDtypeStruct((48, width), BF)] * cols,
        in_specs=[SMEM_SPEC] * 2 + [VMEM_SPEC] * 3,
        out_specs=[VMEM_SPEC] * cols,
        scratch_shapes=[pltpu.VMEM((cols, 48, width), F32), scales, scales],
        name="split",
        compiler_params=pltpu.CompilerParams(vmem_limit_bytes=4 << 20),
    )(where, layer, up, down, sums)
    arrived = [pieces[0]] + [swap(pieces[s], "col", cols, s) for s in range(1, cols)]
    return pl.pallas_call(
        join_kernel,
        out_shape=jax.ShapeDtypeStruct((48, cols * width), BF),
        in_specs=[SMEM_SPEC] + [VMEM_SPEC] * cols,
        out_specs=VMEM_SPEC,
        name="join",
        compiler_params=pltpu.CompilerParams(vmem_limit_bytes=2 << 20),
    )(where, *arrived)


def solution(mesh):
    placed = (
        P("row", "layer", "col", None, None),
        P("row", "layer", "col", None),
        P("row", "layer", "col"),
        P(),
        P("layer", "row", None, "col", None, None),
        P("layer", "row", None, "col", None),
        P("layer", "row", None, "col"),
    )
    return jax.shard_map(
        body,
        mesh=mesh,
        in_specs=placed,
        out_specs=P(("row", "col", "layer"), None),
        check_vma=False,
    )
```

```python
import functools

import jax
import jax.numpy as jnp
from jax import lax
from jax.experimental import pallas as pl
from jax.experimental.pallas import tpu as pltpu
from jax.sharding import PartitionSpec as P

CB = 8
PANEL_ROWS = 8
BF = jnp.bfloat16
F32 = jnp.float32
VMEM_SPEC = pl.BlockSpec(memory_space=pltpu.VMEM)
SMEM_SPEC = pl.BlockSpec(memory_space=pltpu.SMEM)


def expand_kernel(row_ref, *refs):
    p_refs, out_ref = refs[:2], refs[2]
    panels = out_ref.shape[0] // PANEL_ROWS
    for core, p_ref in enumerate(p_refs):
        @pl.loop(0, p_ref.shape[0])
        def _(n):
            expand_panel(p_ref, n, row_ref[0] ^ (2 * n + core), out_ref)

    out_ref[panels * PANEL_ROWS] = jnp.zeros(out_ref.shape[1:], BF)


def expand_panel(p_ref, n, panel, out_ref):
    for w in range(PANEL_ROWS):
        blocks = p_ref[n, w * 64:(w + 1) * 64, :]
        sources, wanted = [], []
        for half in range(2):
            straight = blocks[:, half * 128:(half + 1) * 128]
            swapped = jnp.concatenate([straight[:, 64:], straight[:, :64]], axis=1)
            for side, source in enumerate((straight, swapped)):
                sources.append(source.reshape(4, 16, 128))
                r = PANEL_ROWS * 64 + 2 * w + half
                want = p_ref[n, r:r + 1, side * 128:(side + 1) * 128]
                wanted.append(jnp.broadcast_to(want.astype(F32), (16, 128)))
        for j in range(4):
            total = None
            for source, want in zip(sources, wanted):
                term = source * jnp.where(want == 2.0 * j, 1.0, 0.0).astype(BF)[None]
                total = term if total is None else total + term
            out_ref[panel * PANEL_ROWS + w, j] = total.reshape(64, 128)


def multiply(sums, add, k_ref, dense_ref, lefts):
    for g in range(sums.shape[1]):
        @pl.loop(0, 2)
        def _(h):
            for v in range(3):
                i = g * 6 + h * 3 + v
                left, right = [], []
                for n, (a_ref, base) in enumerate(lefts(g)):
                    for s in range(2):
                        first = ((i - base) * 2 + s) * 64
                        left.append(a_ref[pl.ds(pl.multiple_of(first, 64), 64), :])
                        for slot in range(2):
                            k = k_ref[4 * n + 2 * s + slot, i]
                            right.append(jnp.concatenate([dense_ref[k, j] for j in range(4)], axis=1))
                total = jnp.dot(
                    jnp.concatenate(left, axis=1), jnp.concatenate(right, axis=0), preferred_element_type=F32
                )
                for piece in range(4):
                    row = v * 64 + piece * 16
                    where = (h * 4 + row // 48, g, slice(row % 48, row % 48 + 16))
                    term = total[piece * 16:(piece + 1) * 16]
                    sums[where] = sums[where] + term if add else term


def load_k(k_tiles, k_vector, k_ref, sem):
    for n, k in enumerate(k_tiles):
        k_vector[4 * n:4 * n + 4] = k.astype(F32).astype(jnp.int32)[0:4]
    copy = pltpu.make_async_copy(k_vector, k_ref, sem)
    copy.start()
    copy.wait()


def near_kernel(*refs):
    a_refs, dense_ref, sums, scratch = refs[:3], refs[3], refs[4], refs[5:]
    count = a_refs[0].shape[0] - 16
    load_k([a[count:count + 16] for a in a_refs], *scratch)
    multiply(sums, False, scratch[1], dense_ref, lambda g: [(a, 0) for a in a_refs])


def code(x_of, out, scales):
    scales[...] = jnp.zeros_like(scales)
    for g in range(12):
        x = x_of(g)
        most = jnp.maximum(jnp.max(jnp.abs(x), axis=0, keepdims=True), 1e-33)
        e = jnp.ceil(64.0 * (jnp.log2(most) - 15.0)) + 1.0
        scales[g:g + 1] = e
        out[g * 16:(g + 1) * 16] = jnp.floor(x * jnp.exp2(e * (-1.0 / 64)) + 0.5).astype(jnp.int32).astype(jnp.int16)
    out[192:208] = scales[...].astype(jnp.int32).astype(jnp.int16)


def decoded(ref, scales):
    scales[...] = jnp.exp2(ref[192:208].astype(jnp.int32).astype(F32) * (1.0 / 64))
    return lambda g: ref[g * 16:(g + 1) * 16].astype(jnp.int32).astype(F32) * scales[g:g + 1]


def rows_of(sums, index):
    return lambda g: sums[index, g // 3, (g % 3) * 16:(g % 3) * 16 + 16, :]


def far_kernel(layer_ref, sums_in, first_ref, second_ref, dense_ref, sums, up, down, *scratch):
    count = second_ref.shape[0] - 16
    k_scratch, scales = scratch[:3], scratch[3]
    load_k([second_ref[count:count + 16]], *k_scratch)
    half = sums.shape[1] // 2
    multiply(
        sums, True, k_scratch[1], dense_ref,
        lambda g: [(first_ref, 0) if g < half else (second_ref, 6 * half)],
    )
    layers = sums.shape[0]
    code(rows_of(sums, lax.rem(layer_ref[0] + 4, layers)), up, scales)
    code(rows_of(sums, lax.rem(layer_ref[0] + 5, layers)), down, scales)


def hop_kernel(offset, layer_ref, arrived, sums, out, scales_in, scales):
    mine = rows_of(sums, lax.rem(layer_ref[0] + offset, sums.shape[0]))
    other = decoded(arrived, scales_in)
    code(lambda g: mine(g) + other(g), out, scales)


def split_kernel(here_ref, layer_ref, up, down, sums, *refs):
    outs, (whole, scales_up, scales_down) = refs[:-3], refs[-3:]
    mine = rows_of(sums, layer_ref[0])
    above, below = decoded(up, scales_up), decoded(down, scales_down)
    for g in range(12):
        whole[g // 3, (g % 3) * 16:(g % 3) * 16 + 16] = mine(g) + above(g) + below(g)
    for s, out in enumerate(outs):
        out[...] = whole[here_ref[0] ^ s].astype(BF)


def join_kernel(c_ref, *refs):
    pieces, out = refs[:-1], refs[-1]
    for s, piece in enumerate(pieces):
        width = piece.shape[1]
        source = c_ref[0] ^ s
        out[:, pl.ds(pl.multiple_of(source * width, width), width)] = piece[...]


def swap(x, axis, size, mask):
    return lax.ppermute(x, axis, [(n, n ^ mask) for n in range(size)])


def shift(x, axis, size, by):
    return lax.ppermute(x, axis, [(n, (n + by) % size) for n in range(size)])


def body(a_vals, a_cols, a_count, panel_map, p_vals, p_cols, p_count):
    rows = a_vals.shape[0]
    sections = a_vals.shape[2]
    side = a_vals.shape[3]
    cols, layers, grid_rows = 4, 8, 8
    here = lax.axis_index("col")
    layer = lax.axis_index("layer")
    row = lax.axis_index("row")
    panel_rows = p_vals.shape[2]
    fine = panel_map.shape[1] * panel_rows

    a_flat = a_vals[:, 0].reshape(rows * sections * side, 2 * side)
    p_flat = p_vals.reshape(panel_rows * side, p_cols.shape[4] * side)
    panels = lax.dynamic_slice(panel_map, (layer, here * sections), (1, sections)).reshape(sections, 1, 1)
    slot_a = a_cols.shape[3]
    counts, columns = a_count.transpose(1, 2, 0)[0], a_cols.transpose(1, 2, 3, 0)[0]
    k_index = [
        jnp.where(counts > slot, panels[:, :, 0] * panel_rows + columns[:, slot], fine) for slot in range(slot_a)
    ]
    k_index = jnp.stack(k_index, axis=1).reshape(sections * slot_a, rows)
    k_tile = jnp.pad(k_index.astype(BF), ((0, 16 - sections * slot_a), (0, 2 * side - rows)))
    own = jnp.concatenate([a_flat, k_tile], axis=0)

    from_left, from_right = swap(own, "col", cols, 1), swap(own, "col", cols, 3)

    slot_p = p_cols.shape[4]
    index = jnp.where(jnp.arange(slot_p) < p_count[0, 0, :, 0, None], p_cols[0, 0, :, 0], -9)
    odd = index.reshape(panel_rows, 2, 2)
    odd = jnp.concatenate([odd - jnp.array([0, 1]), odd[:, :, ::-1] - jnp.array([0, 1])], axis=2)
    wanted = jnp.broadcast_to(odd[:, :, :, None].astype(BF), (panel_rows, 2, 4, side))
    mine = jnp.concatenate([p_flat, wanted.reshape(2 * panel_rows, 4 * side)], axis=0)
    p_line = [swap(mine, "row", grid_rows, mask) for mask in (2, 4, 6)]
    cut = a_flat.shape[0] // 2
    halves = [from_right[:cut], from_left[cut:]]
    p_line, halves, from_left, from_right = lax.optimization_barrier((p_line, halves, from_left, from_right))
    far_first, far_second = swap(halves[0], "col", cols, 1), swap(halves[1], "col", cols, 3)
    p_line = jnp.stack([mine] + p_line)
    p_pair = swap(p_line, "row", grid_rows, 1)

    dense = pl.pallas_call(
        expand_kernel,
        out_shape=jax.ShapeDtypeStruct((fine + 1, 4, side, 128), BF),
        in_specs=[SMEM_SPEC] + [VMEM_SPEC] * 2,
        out_specs=VMEM_SPEC,
        name="expand",
        compiler_params=pltpu.CompilerParams(vmem_limit_bytes=14 << 20),
        cost_estimate=pl.CostEstimate(flops=0, bytes_accessed=10 << 20, transcendentals=0),
    )(row.reshape(1), p_line, p_pair)

    width = CB * side
    sums_shape = jax.ShapeDtypeStruct((layers, rows // 6, 48, width), F32)
    coded = jax.ShapeDtypeStruct((208, width), jnp.int16)
    k_scratch = [pltpu.VMEM((16, 128), jnp.int32), pltpu.SMEM((16, 128), jnp.int32), pltpu.SemaphoreType.DMA(())]
    scales = pltpu.VMEM((16, width), F32)
    layer = layer.reshape(1)
    sums = pl.pallas_call(
        near_kernel,
        out_shape=sums_shape,
        in_specs=[VMEM_SPEC] * 4,
        out_specs=VMEM_SPEC,
        scratch_shapes=k_scratch,
        name="near",
        compiler_params=pltpu.CompilerParams(vmem_limit_bytes=14 << 20),
        cost_estimate=pl.CostEstimate(flops=4 << 30, bytes_accessed=11 << 20, transcendentals=0),
    )(own, from_left, from_right, dense)
    sums, up, down = pl.pallas_call(
        far_kernel,
        out_shape=[sums_shape, coded, coded],
        in_specs=[SMEM_SPEC] + [VMEM_SPEC] * 4,
        out_specs=[VMEM_SPEC] * 3,
        scratch_shapes=k_scratch + [scales],
        input_output_aliases={1: 0},
        name="far",
        compiler_params=pltpu.CompilerParams(vmem_limit_bytes=14 << 20),
        cost_estimate=pl.CostEstimate(flops=1 << 30, bytes_accessed=9 << 20, transcendentals=0),
    )(layer, sums, far_first, far_second, dense)

    def hop(offset, arrived):
        return pl.pallas_call(
            functools.partial(hop_kernel, offset),
            out_shape=coded,
            in_specs=[SMEM_SPEC] + [VMEM_SPEC] * 2,
            out_specs=VMEM_SPEC,
            scratch_shapes=[scales, scales],
            name="hop",
            compiler_params=pltpu.CompilerParams(vmem_limit_bytes=4 << 20),
            cost_estimate=pl.CostEstimate(flops=0, bytes_accessed=1 << 20, transcendentals=0),
        )(layer, arrived, sums)

    for step in range(4):
        up = shift(up, "layer", layers, 1)
        if step < 3:
            up = hop(3 - step, up)
            down = shift(down, "layer", layers, -1)
        if step < 2:
            down = hop(6 + step, down)

    where = here.reshape(1)
    pieces = pl.pallas_call(
        split_kernel,
        out_shape=[jax.ShapeDtypeStruct((48, width), BF)] * cols,
        in_specs=[SMEM_SPEC] * 2 + [VMEM_SPEC] * 3,
        out_specs=[VMEM_SPEC] * cols,
        scratch_shapes=[pltpu.VMEM((cols, 48, width), F32), scales, scales],
        name="split",
        compiler_params=pltpu.CompilerParams(vmem_limit_bytes=4 << 20),
    )(where, layer, up, down, sums)
    arrived = [pieces[0]] + [swap(pieces[s], "col", cols, s) for s in range(1, cols)]
    return pl.pallas_call(
        join_kernel,
        out_shape=jax.ShapeDtypeStruct((48, cols * width), BF),
        in_specs=[SMEM_SPEC] + [VMEM_SPEC] * cols,
        out_specs=VMEM_SPEC,
        name="join",
        compiler_params=pltpu.CompilerParams(vmem_limit_bytes=2 << 20),
    )(where, *arrived)


def solution(mesh):
    placed = (
        P("row", "layer", "col", None, None),
        P("row", "layer", "col", None),
        P("row", "layer", "col"),
        P(),
        P("layer", "row", None, "col", None, None),
        P("layer", "row", None, "col", None),
        P("layer", "row", None, "col"),
    )
    return jax.shard_map(
        body,
        mesh=mesh,
        in_specs=placed,
        out_specs=P(("row", "col", "layer"), None),
        check_vma=False,
    )
```
